32 devices in a mesh: branch: 2 (over core), seq: 8 (over z, y), fsdp: 2 (over x).
Axes of the slice: x: 2, y: 2, z: 4, core: 2. Of those that a mesh axis runs over, the one named last changes fastest.
Arguments:
- latents: bfloat16 [1536, 5120], P('seq'), may hold values from -6 to 6
- noise: bfloat16 [2, 1536, 5120], P(None, 'seq'), may hold values from -6 to 6
- time_index: int32 [2], replicated, may hold values from 20 to 979
- cfg_pair: int32 [2], replicated, may hold values from 0 to 15
- cond_table: float32 [16, 5120], replicated, may hold values from -6 to 6
- gain: float32 [2, 5120], P('branch'), may hold values from 0.5 to 1.5
- w_qkv: bfloat16 [2, 3, 5120, 3072], P('branch', None, 'seq', 'fsdp'), may hold values from -0.5 to 0.5
- w_out: bfloat16 [2, 3072, 5120], P('branch', 'fsdp', 'seq'), may hold values from -0.109375 to 0.109375
Outputs:
- dmd_grad: float32 [1536, 5120], P('seq', ('branch', 'fsdp'))
- critic_residual: float32 [1536, 5120], P('seq', ('branch', 'fsdp'))
The draws below stay inside these ranges and needn't reach their ends.
All inputs are finite; a program needn't handle non-finite values.
Results may differ from the reference program's by a relative error of at most 0.013.
Values may be sent and summed in bfloat16 or wider, within the bound.
No kernel may reach another device: no remote copies, remote signals or barrier semaphores. Data moves between devices by JAX's collectives and lax.ppermute only.
A program may use at most 128 MiB of HBM per device.

```python
import jax
import jax.numpy as jnp
from jax import lax

D = 5120
HEADS = 24
HD = 128
NCOND = 16
L = 1536
N_FSDP = 2


def draw_w_qkv(key, part):
    key_base = jax.random.fold_in(jax.random.fold_in(key, 11), 0)
    shape = (2, 3, D, HEADS * HD)
    stacked = jax.random.normal(key_base, shape, jnp.float32)
    return jnp.clip(stacked * D ** (-0.5), -0.5, 0.5).astype(jnp.bfloat16)


def levels(key, dims, pieces, least, largest):
    def one(axis_at, parts):
        steps = jax.random.uniform(jax.random.fold_in(jax.random.fold_in(key, 6), axis_at), (parts,), jnp.float32, least / len(pieces), largest / len(pieces))
        return jnp.repeat(jnp.exp(steps), dims[axis_at] // parts).reshape((-1,) + (1,) * (len(dims) - axis_at - 1))

    factor_of = one(*pieces[0])
    for cut in pieces[1:]:
        factor_of = factor_of * one(*cut)
    return factor_of


def normal_values(rng, shape, width, limit, pieces=(), held_as=jnp.bfloat16):
    array = jax.random.normal(rng, shape, jnp.float32) * width
    if len(pieces) > 0:
        array = levels(rng, shape, pieces, -0.22, 0.18) * array
    return jnp.clip(array, min=-limit, max=limit).astype(held_as)


def setup_inputs(seed: int = 0) -> dict:
    arg_keys = jax.random.split(jax.random.key(seed), 9)
    return {
        "latents": normal_values(arg_keys[0], (L, D), 1.0, 6.0, ((0, 8),)),
        "noise": normal_values(arg_keys[1], (2, L, D), 1.0, 6.0, ((1, 8),)),
        "time_index": jax.random.randint(arg_keys[2], (2,), 20, 980).astype(jnp.int32),
        "cfg_pair": jax.random.randint(arg_keys[3], (2,), 0, NCOND).astype(jnp.int32),
        "cond_table": normal_values(arg_keys[4], (NCOND, D), 1.0, 6.0, (), jnp.float32),
        "gain": jnp.clip(1.0 + 0.1 * jax.random.normal(arg_keys[5], (2, D), jnp.float32), 0.5, 1.5),
        "w_qkv": draw_w_qkv(jax.random.fold_in(arg_keys[8], 71), 0),
        "w_out": normal_values(arg_keys[7], (2, HEADS * HD, D), (HEADS * HD) ** -0.5, 0.109375, ((0, 2), (1, 2), (2, 8))),
    }


GUIDANCE = 3.5
EPSILON = 1e-06

def sigma_of(step_index):
    fraction = step_index.astype(jnp.float32) / 1000.0
    return 5.0 * fraction / (1.0 + 4.0 * fraction)

def noisy_mix(tokens, noise_rows, step_index):
    noise_level = sigma_of(step_index)
    return (1.0 - noise_level) * tokens + noise_level * noise_rows.astype(jnp.float32)

def normed(noisy_rows, gain_row, shift_row):
    mean_square = lax.optimization_barrier(jnp.mean(noisy_rows * noisy_rows, axis=-1, keepdims=True))
    return (noisy_rows * lax.rsqrt(mean_square + EPSILON) * gain_row + shift_row).astype(jnp.bfloat16)

def head_out(operands):
    query_rows, key_rows, value_rows = operands
    scores = jnp.dot(query_rows, key_rows.T, preferred_element_type=jnp.float32) * HD ** (-0.5)
    peak_score = lax.optimization_barrier(jnp.max(scores, axis=1, keepdims=True))
    softmax_w = jnp.exp(scores - peak_score)
    mass_total = lax.optimization_barrier(jnp.sum(softmax_w, axis=1, keepdims=True))
    mixed = jnp.dot(softmax_w.astype(jnp.bfloat16), value_rows, preferred_element_type=jnp.float32)
    return (mixed / mass_total).astype(jnp.bfloat16)

def section(inputs, weights, out_weight):
    seq_len = inputs.shape[0]
    projected = [jnp.dot(inputs, weights[j], preferred_element_type=jnp.float32).astype(jnp.bfloat16) for j in range(3)]
    per_head = [item.reshape(seq_len, HEADS, HD).transpose(1, 0, 2) for item in projected]
    outputs = lax.map(head_out, (per_head[0], per_head[1], per_head[2]))
    attn = outputs.transpose(1, 0, 2).reshape(seq_len, HEADS * HD)
    col_width = HEADS * HD // N_FSDP
    summed = jnp.zeros((seq_len, out_weight.shape[1]), jnp.float32)
    for group in range(N_FSDP):
        head_part = jnp.dot(attn[:, group * col_width:(group + 1) * col_width], out_weight[group * col_width:(group + 1) * col_width], preferred_element_type=jnp.float32)
        head_part = lax.optimization_barrier(head_part.astype(jnp.bfloat16)).astype(jnp.float32)
        summed = summed + head_part
    return summed

def reference(latents, noise, time_index, cfg_pair, cond_table, gain, w_qkv, w_out):
    tokens = latents.astype(jnp.float32)
    noisy_main = noisy_mix(tokens, noise[0], time_index[0])
    noisy_own = noisy_mix(tokens, noise[1], time_index[1])
    cond_row = cond_table[cfg_pair[0]]
    null_row = cond_table[cfg_pair[1]]
    teacher_cond = section(normed(noisy_main, gain[0], cond_row), w_qkv[0], w_out[0])
    teacher_null = section(normed(noisy_main, gain[0], null_row), w_qkv[0], w_out[0])
    critic_main = section(normed(noisy_main, gain[1], cond_row), w_qkv[1], w_out[1])
    critic_own = section(normed(noisy_own, gain[1], cond_row), w_qkv[1], w_out[1])
    dmd_grad = critic_main - (teacher_null + GUIDANCE * (teacher_cond - teacher_null))
    critic_residual = critic_own - (noise[1].astype(jnp.float32) - tokens)
    return (dmd_grad, critic_residual)
```

```python
import functools
import math

import jax
import jax.numpy as jnp
from jax import lax
from jax.experimental import pallas as pl
from jax.experimental.pallas import tpu as pltpu
from jax.sharding import Mesh
from jax.sharding import PartitionSpec as P

HD = 128
GUIDANCE = 3.5
EPSILON = 1e-06


def sigma_of(step_index):
    fraction = step_index.astype(jnp.float32) / 1000.0
    return 5.0 * fraction / (1.0 + 4.0 * fraction)


def noisy_mix(tokens, noise_rows, step_index):
    noise_level = sigma_of(step_index)
    return (1.0 - noise_level) * tokens + noise_level * noise_rows.astype(jnp.float32)


def table_row(cond_table, cond_row):
    one_hot = (jnp.arange(cond_table.shape[0], dtype=jnp.int32) == cond_row).astype(jnp.float32)
    return jnp.dot(one_hot, cond_table, precision=lax.Precision.HIGHEST)


def swap(x, axis):
    return lax.ppermute(x, axis, [(0, 1), (1, 0)])


def shift(x, axis, distance):
    size = lax.axis_size(axis)
    return lax.ppermute(x, axis, [(i, (i + distance) % size) for i in range(size)])


def attend_kernel(q_ref, k0_ref, v0_ref, k1_ref, v1_ref, o_ref):
    q = q_ref[0]
    dims = (((1,), (1,)), ((), ()))
    scale = HD ** (-0.5)
    s0 = lax.dot_general(q, k0_ref[0], dims, preferred_element_type=jnp.float32) * scale
    s1 = lax.dot_general(q, k1_ref[0], dims, preferred_element_type=jnp.float32) * scale
    peak = jnp.maximum(
        jnp.max(s0, axis=1, keepdims=True), jnp.max(s1, axis=1, keepdims=True)
    )
    p0 = jnp.exp(s0 - peak)
    p1 = jnp.exp(s1 - peak)
    mass = jnp.sum(p0, axis=1, keepdims=True) + jnp.sum(p1, axis=1, keepdims=True)
    mixed = jnp.dot(p0.astype(jnp.bfloat16), v0_ref[0], preferred_element_type=jnp.float32)
    mixed += jnp.dot(p1.astype(jnp.bfloat16), v1_ref[0], preferred_element_type=jnp.float32)
    o_ref[0] = (mixed / mass).astype(jnp.bfloat16)


def attend(q, k0, v0, k1, v1):
    passes, rows, _ = q.shape
    tile = 256 if rows % 256 == 0 else rows
    q_spec = pl.BlockSpec((1, tile, HD), lambda p, t: (p, t, 0))
    kv_spec = pl.BlockSpec((1, k0.shape[1], HD), lambda p, t: (p, 0, 0))
    return pl.pallas_call(
        attend_kernel,
        name="attend",
        grid=(passes, rows // tile),
        in_specs=[q_spec] + [kv_spec] * 4,
        out_specs=q_spec,
        out_shape=jax.ShapeDtypeStruct(q.shape, jnp.bfloat16),
        cost_estimate=pl.CostEstimate(
            flops=8 * passes * rows * k0.shape[1] * HD,
            transcendentals=2 * passes * rows * k0.shape[1],
            bytes_accessed=2 * (2 * q.size + 4 * k0.size),
        ),
    )(q, k0, v0, k1, v1)


def project_out_kernel(first, *refs):
    if first:
        a_ref, w_ref, o_ref = refs
    else:
        a_ref, w_ref, c_ref, o_ref = refs
    rows = jnp.concatenate([a_ref[i, 0] for i in range(a_ref.shape[0])], axis=1)
    total = jnp.dot(rows, w_ref[...], preferred_element_type=jnp.float32)
    o_ref[0] = total if first else c_ref[0] + total


def project_out(attn, weight, carry):
    groups, passes, rows, _ = attn.shape
    width = weight.shape[1]
    tile = 256 if rows % 256 == 0 else rows
    o_spec = pl.BlockSpec((1, tile, width), lambda p, t: (p, t, 0))
    first = carry is None
    return pl.pallas_call(
        functools.partial(project_out_kernel, first),
        name="project_out",
        grid=(passes, rows // tile),
        in_specs=[
            pl.BlockSpec((groups, 1, tile, HD), lambda p, t: (0, p, t, 0)),
            pl.BlockSpec(weight.shape, lambda p, t: (0, 0)),
        ]
        + ([] if first else [o_spec]),
        out_specs=o_spec,
        out_shape=jax.ShapeDtypeStruct((passes, rows, width), jnp.float32),
        cost_estimate=pl.CostEstimate(
            flops=2 * passes * rows * weight.size,
            transcendentals=0,
            bytes_accessed=2 * attn.size + 2 * weight.size + 8 * passes * rows * width,
        ),
    )(*((attn, weight) if first else (attn, weight, carry)))


def split_body(latents, noise, time_index, cfg_pair, cond_table, gain, w_qkv, w_out):
    b = lax.axis_index("branch")
    z = lax.axis_index("outer")
    y = lax.axis_index("inner")
    f = lax.axis_index("fsdp")
    nz = lax.axis_size("outer")
    nf = lax.axis_size("fsdp")
    tok, width = latents.shape
    half = width // nf
    weights = w_qkv[0]
    d_rows, cols = weights.shape[1:]
    head_count = cols // HD // nz

    def cut(distance, head):
        start = ((z + distance) % nz * head_count + head) * HD
        return lax.dynamic_slice_in_dim(weights, start, HD, 2)

    def place(buffer, block, z_from, y_from):
        at = (z_from * 2 + y_from - f * (nz * 2 // nf)) % (nz * 2)
        return lax.dynamic_update_slice(buffer, block, (0, at * d_rows, 0))

    head_weights = []
    gate = None
    for head in range(head_count):
        buffer = jnp.zeros((3, width, HD), jnp.bfloat16)
        sends = [cut(distance, head) for distance in range(nz)]
        if gate is not None:
            *sends, _ = lax.optimization_barrier((*sends, gate))
        received = [sends[0]] + [shift(sends[d], "outer", d) for d in range(1, nz)]
        gate = received[1]
        for d in range(nz):
            z_from = (z - d) % nz
            buffer = place(buffer, received[d], z_from, y)
            buffer = place(buffer, swap(received[d], "inner"), z_from, 1 - y)
        head_weights.append(buffer)

    tokens = latents.astype(jnp.float32)
    own_noise = lax.dynamic_index_in_dim(noise, b, 0, keepdims=False)
    own_index = lax.dynamic_index_in_dim(time_index, b, 0, keepdims=False)
    noisy = noisy_mix(tokens, own_noise, own_index)
    mean_square = jnp.mean(noisy * noisy, axis=-1, keepdims=True)
    unit = (noisy * lax.rsqrt(mean_square + EPSILON)).astype(jnp.bfloat16)
    mine = lax.dynamic_slice_in_dim(unit, f * half, half, 1)
    mine = lax.all_gather(mine, "outer", axis=0, tiled=True)
    theirs = swap(mine, "fsdp")
    own_rows = jnp.concatenate([mine, theirs], axis=1)
    main_rows = lax.ppermute(own_rows, "branch", [(0, 1)])
    main_rows = jnp.where(b == 0, own_rows, main_rows)

    def turned(vector):
        return lax.dynamic_slice_in_dim(jnp.concatenate([vector, vector]), f * half, width, 0)

    gain_row = turned(gain[0])
    cond_shift = turned(table_row(cond_table, cfg_pair[0]))
    second_row = lax.dynamic_index_in_dim(cfg_pair, 1 - b, 0, keepdims=False)
    second_shift = turned(table_row(cond_table, second_row))
    inputs = jnp.stack(
        [
            (main_rows.astype(jnp.float32) * gain_row + cond_shift).astype(jnp.bfloat16),
            (own_rows.astype(jnp.float32) * gain_row + second_shift).astype(jnp.bfloat16),
        ]
    )

    out_a = lax.ppermute(
        w_out[0], ("inner", "fsdp"), [(yy * 2 + ff, ff * 2 + yy) for yy in (0, 1) for ff in (0, 1)]
    )
    out_b = lax.ppermute(
        w_out[0],
        ("inner", "fsdp"),
        [(yy * 2 + ff, (1 - ff) * 2 + yy) for yy in (0, 1) for ff in (0, 1)],
    )
    out_width = out_a.shape[1]
    out_weights = jnp.stack([jnp.where(y == 0, out_a, out_b), jnp.where(y == 0, out_b, out_a)])
    out_weights = out_weights.reshape(nf, nz, head_count, HD, out_width).transpose(2, 1, 0, 3, 4)
    out_weights = out_weights.reshape(head_count, nz * nf * HD, out_width)

    pred = None
    for head in range(head_count):
        projected = jnp.einsum(
            "ptd,jdc->jptc", inputs, head_weights[head], preferred_element_type=jnp.float32
        ).astype(jnp.bfloat16)
        pair = projected[1:]
        other = swap(pair, "inner")
        attn = attend(projected[0], pair[0], pair[1], other[0], other[1])
        gathered = lax.all_gather(attn, ("outer", "fsdp"), axis=0)
        pred = project_out(gathered, out_weights[head], pred)

    critic_main = lax.ppermute(pred[0], "branch", [(1, 0)])
    dmd = critic_main - (pred[1] + GUIDANCE * (pred[0] - pred[1]))
    value = jnp.where(b == 0, dmd, pred[1]).astype(jnp.bfloat16)
    value = value.reshape(nz, tok, out_width)
    received = []
    axes = ("branch", "outer", "fsdp")
    for k in range(nz):
        pairs = []
        for bb in range(2):
            for zz in range(nz):
                for ff in range(nf):
                    to = (bb * nf + ff + k) % nz
                    source = (bb * nz + zz) * nf + ff
                    target = (zz // nf * nz + to) * nf + zz % nf
                    pairs.append((source, target))
        block = lax.dynamic_index_in_dim(value, (b * nf + f + k) % nz, 0, keepdims=False)
        received.append(lax.ppermute(block, axes, pairs))
    received = jnp.stack(received)
    ordered = [
        lax.dynamic_index_in_dim(received, (z - m) % nz, 0, keepdims=False) for m in range(nz)
    ]
    dmd_grad = jnp.concatenate(ordered[:nf], axis=1).astype(jnp.float32)
    own_pred = jnp.concatenate(ordered[nf:], axis=1).astype(jnp.float32)
    out_cols = out_width * nf
    col_start = (b * nf + f) * out_cols
    noise_cols = lax.dynamic_slice_in_dim(noise[1], col_start, out_cols, 1).astype(jnp.float32)
    latent_cols = lax.dynamic_slice_in_dim(latents, col_start, out_cols, 1).astype(jnp.float32)
    return (dmd_grad, own_pred - (noise_cols - latent_cols))


def attend_all(queries, key_rows, value_rows):
    passes, key_count = (key_rows.shape[0], key_rows.shape[1])
    local_heads = queries.shape[2]
    key_rows = key_rows.reshape(passes, key_count, local_heads, HD)
    value_rows = value_rows.reshape(passes, key_count, local_heads, HD)
    scores = jnp.einsum(
        "pqhd,prhd->pqhr", queries, key_rows, preferred_element_type=jnp.float32
    ) * HD ** (-0.5)
    softmax_w = jnp.exp(scores - jnp.max(scores, axis=-1, keepdims=True))
    mass = jnp.sum(softmax_w, axis=-1)
    mixed = jnp.einsum(
        "pqhr,prhd->pqhd",
        softmax_w.astype(jnp.bfloat16),
        value_rows,
        preferred_element_type=jnp.float32,
    )
    return (mixed / mass[..., None]).astype(jnp.bfloat16)


def normed(noisy_rows, gain_row, shift_row):
    mean_square = jnp.mean(noisy_rows * noisy_rows, axis=-1, keepdims=True)
    return (noisy_rows * lax.rsqrt(mean_square + EPSILON) * gain_row + shift_row).astype(
        jnp.bfloat16
    )


def gathered_body(latents, noise, time_index, cfg_pair, cond_table, gain, w_qkv, w_out):
    branch = lax.axis_index("branch")
    fsdp_count = lax.axis_size("fsdp")
    tok_rows = latents.shape[0]
    tokens = latents.astype(jnp.float32)
    noisy_main = noisy_mix(tokens, noise[0], time_index[0])
    own_noise = lax.dynamic_index_in_dim(noise, branch, 0, keepdims=False)
    own_index = lax.dynamic_index_in_dim(time_index, branch, 0, keepdims=False)
    noisy_own = noisy_mix(tokens, own_noise, own_index)
    cond_shift = table_row(cond_table, cfg_pair[0])
    second_row = lax.dynamic_index_in_dim(cfg_pair, 1 - branch, 0, keepdims=False)
    second_shift = table_row(cond_table, second_row)
    gain_row = gain[0]
    inputs = jnp.stack(
        [normed(noisy_main, gain_row, cond_shift), normed(noisy_own, gain_row, second_shift)]
    )
    weights = w_qkv[0]
    col_count = weights.shape[2]
    local_heads = col_count // HD
    projected = jnp.einsum(
        "ptd,jdc->pjtc",
        inputs,
        lax.all_gather(weights, "seq", axis=1, tiled=True),
        preferred_element_type=jnp.float32,
    ).astype(jnp.bfloat16)
    attn = attend_all(
        projected[:, 0].reshape(2, tok_rows, local_heads, HD),
        lax.all_gather(projected[:, 1], "seq", axis=1, tiled=True),
        lax.all_gather(projected[:, 2], "seq", axis=1, tiled=True),
    ).reshape(2, tok_rows, col_count)
    partial_value = jnp.einsum(
        "ptc,cd->ptd",
        attn,
        lax.all_gather(w_out[0], "seq", axis=1, tiled=True),
        preferred_element_type=jnp.float32,
    )
    width_all = partial_value.shape[2]
    half_width = width_all // (2 * fsdp_count)
    partial_value = (
        partial_value.reshape(2, tok_rows, 2, fsdp_count, half_width)
        .transpose(0, 1, 3, 2, 4)
        .reshape(2, tok_rows, width_all)
    )
    head_sums = lax.psum_scatter(
        partial_value.astype(jnp.bfloat16), "fsdp", scatter_dimension=2, tiled=True
    ).astype(jnp.float32)
    own_half = lax.dynamic_slice_in_dim(head_sums, branch * half_width, half_width, 2)
    give_half = lax.dynamic_slice_in_dim(head_sums, (1 - branch) * half_width, half_width, 2)
    partner_half = swap(give_half.astype(jnp.bfloat16), "branch").astype(jnp.float32)
    is_teacher = branch == 0
    teacher = jnp.where(is_teacher, own_half, partner_half)
    critic = jnp.where(is_teacher, partner_half, own_half)
    dmd_grad = critic[0] - (teacher[1] + GUIDANCE * (teacher[0] - teacher[1]))
    col_start = (branch * fsdp_count + lax.axis_index("fsdp")) * half_width
    noise_cols = lax.dynamic_slice_in_dim(noise[1], col_start, half_width, 1).astype(jnp.float32)
    latent_cols = lax.dynamic_slice_in_dim(latents, col_start, half_width, 1).astype(jnp.float32)
    return (dmd_grad, critic[1] - (noise_cols - latent_cols))


def solution(mesh):
    sizes = dict(mesh.shape)
    branches, seq, fsdp = sizes["branch"], sizes["seq"], sizes["fsdp"]

    def run(latents, noise, time_index, cfg_pair, cond_table, gain, w_qkv, w_out):
        local_heads = w_qkv.shape[3] // HD // fsdp
        outer = math.gcd(local_heads, seq)
        split = outer == branches * fsdp and seq == 2 * outer and branches == 2 and fsdp == 2
        if split:
            used = Mesh(
                mesh.devices.reshape(branches, outer, 2, fsdp),
                ("branch", "outer", "inner", "fsdp"),
            )
            body, along = split_body, ("outer", "inner")
        else:
            used, body, along = mesh, gathered_body, "seq"
        out = P(along, ("branch", "fsdp"))
        return jax.shard_map(
            body,
            mesh=used,
            in_specs=(
                P(along, None),
                P(None, along, None),
                P(),
                P(),
                P(),
                P("branch", None),
                P("branch", None, along, "fsdp"),
                P("branch", "fsdp", along),
            ),
            out_specs=(out, out),
            check_vma=False,
        )(latents, noise, time_index, cfg_pair, cond_table, gain, w_qkv, w_out)

    return run
```

```python
import functools
import math

import jax
import jax.numpy as jnp
from jax import lax
from jax.experimental import pallas as pl
from jax.experimental.pallas import tpu as pltpu
from jax.sharding import Mesh
from jax.sharding import PartitionSpec as P


HD = 128
GUIDANCE = 3.5
EPSILON = 1e-06


def sigma_of(step_index):
    fraction = step_index.astype(jnp.float32) / 1000.0
    return 5.0 * fraction / (1.0 + 4.0 * fraction)


def noisy_mix(tokens, noise_rows, step_index):
    noise_level = sigma_of(step_index)
    return (1.0 - noise_level) * tokens + noise_level * noise_rows.astype(jnp.float32)


def table_row(cond_table, cond_row):
    one_hot = (jnp.arange(cond_table.shape[0], dtype=jnp.int32) == cond_row).astype(jnp.float32)
    return jnp.dot(one_hot, cond_table, precision=lax.Precision.HIGHEST)


def swap(x, axis):
    return lax.ppermute(x, axis, [(0, 1), (1, 0)])


def shift(x, axis, distance):
    size = lax.axis_size(axis)
    return lax.ppermute(x, axis, [(i, (i + distance) % size) for i in range(size)])


def prepare_kernel(b_ref, at_ref, time_ref, latents_ref, noise_ref, *refs):
    *out_refs, held_ref = refs
    _, width = latents_ref.shape
    blocks = at_ref.shape[0]
    step = jnp.full((1, HD), time_ref[b_ref[0]], jnp.int32)
    level = sigma_of(step)[:, :1]
    noisy = (1.0 - level) * latents_ref[...].astype(jnp.float32)
    noisy += level * noise_ref[0].astype(jnp.float32)
    mean_square = jnp.mean(noisy * noisy, axis=1, keepdims=True)
    held_ref[...] = noisy * lax.rsqrt(mean_square + EPSILON)
    size = width // blocks
    each = blocks // len(out_refs)
    for p in range(blocks):
        at = pl.multiple_of(at_ref[p] * size, HD)
        to = slice(p % each * size, (p % each + 1) * size)
        out_refs[p // each][:, to] = held_ref[:, pl.ds(at, size)].astype(jnp.bfloat16)


def prepare(b, order, time_index, latents, noise):
    tok, width = latents.shape
    tile = tok // 2 if tok % 32 == 0 else tok
    rows = pl.BlockSpec((tile, width), lambda t, *_: (t, 0))
    return pl.pallas_call(
        prepare_kernel,
        name="prepare",
        grid_spec=pltpu.PrefetchScalarGridSpec(
            num_scalar_prefetch=3,
            grid=(tok // tile,),
            in_specs=[rows, pl.BlockSpec((1, tile, width), lambda t, b, *_: (b[0], t, 0))],
            out_specs=[pl.BlockSpec((tile, width // 2), lambda t, *_: (t, 0))] * 2,
            scratch_shapes=[pltpu.VMEM((tile, width), jnp.float32)],
        ),
        out_shape=[jax.ShapeDtypeStruct((tok, width // 2), jnp.bfloat16)] * 2,
        cost_estimate=pl.CostEstimate(
            flops=6 * tok * width, transcendentals=tok, bytes_accessed=6 * tok * width
        ),
    )(b, order, time_index, latents, noise)


def affine_kernel(b_ref, at_ref, cfg_ref, own_ref, main_ref, gain_ref, table_ref, o_ref):
    b = b_ref[0]
    gain_row = gain_ref[...]
    own = own_ref[...]
    main = jnp.where(b == 0, own, main_ref[...]).astype(jnp.float32)
    cond = table_ref[pl.ds(cfg_ref[0], 1), :]
    second = table_ref[pl.ds(cfg_ref[1 - b], 1), :]
    o_ref[0] = (main * gain_row + cond).astype(jnp.bfloat16)
    o_ref[1] = (own.astype(jnp.float32) * gain_row + second).astype(jnp.bfloat16)


def affine(b, order, cfg_pair, own_rows, main_rows, gain, table):
    rows, width = own_rows.shape
    blocks = order.shape[0]
    size = width // blocks
    table = table.astype(jnp.float32)
    block = pl.BlockSpec((rows, size), lambda p, *_: (0, p))
    return pl.pallas_call(
        affine_kernel,
        name="affine",
        grid_spec=pltpu.PrefetchScalarGridSpec(
            num_scalar_prefetch=3,
            grid=(blocks,),
            in_specs=[
                block,
                block,
                pl.BlockSpec((1, size), lambda p, b, at, cfg: (0, at[p])),
                pl.BlockSpec((table.shape[0], size), lambda p, b, at, cfg: (0, at[p])),
            ],
            out_specs=pl.BlockSpec((2, rows, size), lambda p, *_: (0, 0, p)),
        ),
        out_shape=jax.ShapeDtypeStruct((2, rows, width), jnp.bfloat16),
        cost_estimate=pl.CostEstimate(
            flops=4 * rows * width, transcendentals=0, bytes_accessed=8 * rows * width
        ),
    )(b, order, cfg_pair, own_rows, main_rows, gain, table)


def project_kernel(place_ref, mine_ref, theirs_ref, *refs):
    blocks, (q_ref, kv_ref) = refs[:-2], refs[-2:]
    total = None
    for d in range(len(blocks) // 2):
        pair = blocks[2 * d : 2 * d + 2]
        weight = jnp.concatenate(
            [jnp.concatenate([w[j] for j in range(3)], axis=1) for w in pair], axis=0
        )
        depth = weight.shape[0]
        each = mine_ref.shape[2] // depth
        here = pl.ds(pl.multiple_of(place_ref[d] % each * depth, HD), depth)
        rows = jnp.where(place_ref[d] < each, mine_ref[0, :, here], theirs_ref[0, :, here])
        part = jnp.dot(rows, weight, preferred_element_type=jnp.float32)
        total = part if total is None else total + part
    total = total.astype(jnp.bfloat16)
    q_ref[0] = total[:, :HD]
    kv_ref[0] = total[:, HD:]


def project(mine, theirs, places, weights, own_swapped, pieces, head):
    passes, rows, half = mine.shape
    width = 2 * half
    depth = weights.shape[1]
    tile = rows // 2 if rows % 32 == 0 else rows
    whole = pl.BlockSpec((3, depth, HD), lambda p, t, at: (0, 0, 0))
    return pl.pallas_call(
        project_kernel,
        name="project",
        grid_spec=pltpu.PrefetchScalarGridSpec(
            num_scalar_prefetch=1,
            grid=(passes, rows // tile),
            in_specs=[
                pl.BlockSpec((1, tile, half), lambda p, t, at: (p, t, 0)),
                pl.BlockSpec((1, tile, half), lambda p, t, at: (p, t, 0)),
                pl.BlockSpec((3, depth, HD), lambda p, t, at: (0, 0, at[at.shape[0] - 1] + head)),
                pl.BlockSpec((3, depth, HD), lambda p, t, at: (0, 0, head)),
            ]
            + [whole] * len(pieces),
            out_specs=[
                pl.BlockSpec((1, tile, HD), lambda p, t, at: (p, t, 0)),
                pl.BlockSpec((1, tile, 2 * HD), lambda p, t, at: (p, t, 0)),
            ],
        ),
        out_shape=[
            jax.ShapeDtypeStruct((passes, rows, HD), jnp.bfloat16),
            jax.ShapeDtypeStruct((passes, rows, 2 * HD), jnp.bfloat16),
        ],
        cost_estimate=pl.CostEstimate(
            flops=6 * passes * rows * width * HD,
            transcendentals=0,
            bytes_accessed=2 * (passes * rows * (width + 3 * HD) + 3 * width * HD),
        ),
    )(places, mine, theirs, weights, own_swapped, *pieces)


def attend_kernel(b_ref, q_ref, own_ref, other_ref, o_ref, give_ref):
    dims = (((1,), (1,)), ((), ()))
    scale = HD ** (-0.5)
    tile = q_ref.shape[1]
    step, steps = pl.program_id(0), pl.num_programs(0)
    mixed = []
    for p in range(2):
        q, own, other = q_ref[p], own_ref[p], other_ref[p]
        s0 = lax.dot_general(q, own[:, :HD], dims, preferred_element_type=jnp.float32) * scale
        s1 = lax.dot_general(q, other[:, :HD], dims, preferred_element_type=jnp.float32) * scale
        peak = jnp.maximum(
            jnp.max(s0, axis=1, keepdims=True), jnp.max(s1, axis=1, keepdims=True)
        )
        p0 = jnp.exp(s0 - peak)
        p1 = jnp.exp(s1 - peak)
        mass = jnp.sum(p0, axis=1, keepdims=True) + jnp.sum(p1, axis=1, keepdims=True)
        total = jnp.dot(p0.astype(jnp.bfloat16), own[:, HD:], preferred_element_type=jnp.float32)
        total += jnp.dot(
            p1.astype(jnp.bfloat16), other[:, HD:], preferred_element_type=jnp.float32
        )
        mixed.append(total / mass)
    teacher = b_ref[0] == 0
    main = jnp.where(teacher, mixed[1] + GUIDANCE * (mixed[0] - mixed[1]), mixed[0])
    second = mixed[1].astype(jnp.bfloat16)
    o_ref[pl.ds(step * tile, tile), :] = main.astype(jnp.bfloat16)

    @pl.when(step < steps // 2)
    def _():
        give_ref[pl.ds(step * tile, tile), :] = second

    @pl.when(step >= steps // 2)
    def _():
        o_ref[pl.ds((step + steps // 2) * tile, tile), :] = second


def attend(b, q, own, other):
    passes, rows, _ = q.shape
    keys = own.shape[1] + other.shape[1]
    tile = rows // 4 if rows % 64 == 0 else rows // 2
    kv_spec = pl.BlockSpec((passes, own.shape[1], 2 * HD), lambda t, b: (0, 0, 0))
    return pl.pallas_call(
        attend_kernel,
        name="attend",
        grid_spec=pltpu.PrefetchScalarGridSpec(
            num_scalar_prefetch=1,
            grid=(rows // tile,),
            in_specs=[
                pl.BlockSpec((passes, tile, HD), lambda t, b: (0, t, 0)),
                kv_spec,
                kv_spec,
            ],
            out_specs=[
                pl.BlockSpec((rows * 3 // 2, HD), lambda t, b: (0, 0)),
                pl.BlockSpec((rows // 2, HD), lambda t, b: (0, 0)),
            ],
        ),
        out_shape=[
            jax.ShapeDtypeStruct((rows * 3 // 2, HD), jnp.bfloat16),
            jax.ShapeDtypeStruct((rows // 2, HD), jnp.bfloat16),
        ],
        cost_estimate=pl.CostEstimate(
            flops=4 * passes * rows * keys * HD,
            transcendentals=passes * rows * keys,
            bytes_accessed=2 * (2 * q.size + 2 * own.size),
        ),
    )(b, q, own, other)


def project_out_kernel(count, first, at_ref, *refs):
    pieces, weights, refs = refs[:count], refs[count : 2 * count], refs[2 * count :]
    rows = jnp.concatenate([a[...] for a in pieces], axis=1)
    weight = jnp.concatenate([w[0] for w in weights], axis=0)
    total = jnp.dot(rows, weight, preferred_element_type=jnp.float32)
    refs[-1][...] = total if first else refs[0][...] + total


def project_out(sets, tiles, places, mine, theirs, carry):
    tile = sets[0][1][0].shape[0] // 3
    each = len(sets[0][1]) // 2
    count = 2 * each * len(sets)
    width = mine.shape[2]
    lo, hi = tiles
    rows = (hi - lo) * tile
    first = carry is None

    def weight_spec(k, head):
        return pl.BlockSpec((1, HD, width), lambda t, at: ((t + lo) // 2, at[k] + head, 0))

    return pl.pallas_call(
        functools.partial(project_out_kernel, count, first),
        name="project_out",
        grid_spec=pltpu.PrefetchScalarGridSpec(
            num_scalar_prefetch=1,
            grid=(hi - lo,),
            in_specs=[pl.BlockSpec((tile, HD), lambda t, at: (t + lo, 0))] * count
            + [weight_spec(k % each, head) for head, _ in sets for k in range(2 * each)]
            + ([] if first else [pl.BlockSpec((tile, width), lambda t, at: (t + lo, 0))]),
            out_specs=pl.BlockSpec((tile, width), lambda t, at: (t, 0)),
        ),
        out_shape=jax.ShapeDtypeStruct((rows, width), jnp.float32),
        cost_estimate=pl.CostEstimate(
            flops=2 * rows * width * HD * count,
            transcendentals=0,
            bytes_accessed=2 * HD * count * (rows + width) + 8 * rows * width,
        ),
    )(
        places,
        *[piece for _, pieces in sets for piece in pieces],
        *(([mine] * each + [theirs] * each) * len(sets)),
        *([] if first else [carry]),
    )


def split_body(*operands):
    return split_step(*operands)


def split_step(latents, noise, time_index, cfg_pair, cond_table, gain, w_qkv, w_out):
    b = lax.axis_index("branch")
    z = lax.axis_index("outer")
    y = lax.axis_index("inner")
    f = lax.axis_index("fsdp")
    nz = lax.axis_size("outer")
    nf = lax.axis_size("fsdp")
    tok, width = latents.shape
    half = width // nf
    weights = w_qkv[0]
    _, cols = weights.shape[1:]
    head_count = cols // HD // nz

    span = head_count * HD
    own_swapped = swap(lax.dynamic_slice_in_dim(weights, z * span, span, 2), "inner")
    head_pieces = []
    for head in range(head_count):
        pieces = []
        for d in range(1, nz):
            start = (z + d) % nz * span + head * HD
            send = lax.dynamic_slice_in_dim(weights, start, HD, 2)
            received = shift(send, "outer", d)
            pieces += [received, swap(received, "inner")]
        head_pieces.append(pieces)
    from_z = jnp.stack([(z - d) % nz for d in range(nz)])
    places = jnp.concatenate([(from_z - 2 * f) % nz, (z * head_count)[None]]).astype(jnp.int32)

    which = b[None].astype(jnp.int32)
    order = jnp.stack(
        [(p // 2 + f * (nz // nf)) % nz * 2 + (y ^ (p % 2)) for p in range(2 * nz)]
    ).astype(jnp.int32)
    unit = prepare(which, order, time_index, latents, noise)
    ups = downs = [(unit[0], None)]
    for k in range(1, nz):
        up = lax.ppermute(ups[-1][0], "outer", [(i, i + 1) for i in range(k - 1, nz - 1)])
        down = lax.ppermute(downs[-1][0], "outer", [(i, i - 1) for i in range(1, nz - k + 1)])
        pairs = [(i * nf + j, i * nf + 1 - j) for i in range(nz) for j in range(nf)]
        ups = ups + [(up, lax.ppermute(up, ("outer", "fsdp"), pairs[k * nf :]))]
        downs = downs + [(down, lax.ppermute(down, ("outer", "fsdp"), pairs[: -k * nf]))]
    inputs = []
    for side in range(2):
        own_rows = jnp.zeros((nz * tok, half), jnp.bfloat16)
        own_rows = lax.dynamic_update_slice(own_rows, unit[side], (z * tok, 0))
        for k in range(1, nz):
            block = jnp.where(z + k < nz, downs[k][side], ups[nz - k][side])
            own_rows = lax.dynamic_update_slice(own_rows, block, ((z + k) % nz * tok, 0))
        main_rows = lax.ppermute(own_rows, "branch", [(0, 1)])
        part = order[side * nz : (side + 1) * nz]
        inputs.append(affine(which, part, cfg_pair, own_rows, main_rows, gain, cond_table))

    out_here = w_out[0]
    out_width = out_here.shape[1]
    out_there = swap(out_here, "inner")
    out_mine = jnp.where(f == y, out_here, out_there)
    out_theirs = swap(jnp.where(f == y, out_there, out_here), "fsdp")
    out_own = jnp.stack([out_mine, out_theirs])
    out_critic = lax.ppermute(out_own, "branch", [(1, 0)])
    out_critic = jnp.where(b == 0, out_critic, out_own)
    out_pairs = jnp.stack([out_own, out_critic], axis=1)
    out_mine, out_theirs = out_pairs[0], out_pairs[1]
    out_places = (from_z * head_count).astype(jnp.int32)

    rows = nz * tok
    sets = []
    for head in range(head_count):
        q, pair = project(*inputs, places, weights, own_swapped, head_pieces[head], head)
        other = swap(pair, "inner")
        attn, give = attend(which, q, pair, other)
        taken = lax.ppermute(give, "branch", [(1, 0)])
        attn = lax.dynamic_update_slice(attn, jnp.where(b == 0, taken, attn[rows:]), (rows, 0))
        ours, across = [attn], [swap(attn, "fsdp")]
        for _ in range(1, nz):
            ours.append(shift(ours[-1], "outer", 1))
            across.append(swap(ours[-1], "fsdp"))
        sets.append((head, ours + across))
    last = (out_places, out_mine, out_theirs)
    early = project_out(sets[:-1], (0, 3), *last, None)
    pred = project_out(sets[-1:], (0, 2), *last, early)
    own_pred = project_out(sets[-1:], (2, 3), *last, early)

    kept = lax.dynamic_slice_in_dim(pred, b * (rows // 2), rows // 2, 0)
    given = lax.dynamic_slice_in_dim(pred, (1 - b) * (rows // 2), rows // 2, 0)
    given = swap(given, "branch")
    dmd = jnp.where(b == 0, given - kept, kept - given)
    value = jnp.stack([dmd, own_pred]).astype(jnp.bfloat16)
    value = value.reshape(2, nz // 2, tok, out_width)
    received = []
    axes = ("branch", "outer", "fsdp")
    for k in range(nz // 2):
        pairs = []
        for bb in range(2):
            for zz in range(nz):
                for ff in range(nf):
                    to = bb * (nz // 2) + (ff + k) % (nz // 2)
                    source = (bb * nz + zz) * nf + ff
                    target = (zz // nf * nz + to) * nf + zz % nf
                    pairs.append((source, target))
        block = lax.dynamic_index_in_dim(value, (f + k) % (nz // 2), 1, keepdims=False)
        received.append(lax.ppermute(block, axes, pairs))
    swapped = z % (nz // 2) == 1
    first = jnp.where(swapped, received[1], received[0])
    second = jnp.where(swapped, received[0], received[1])
    done = jnp.concatenate([first, second], axis=2).astype(jnp.float32)
    out_cols = out_width * nf
    col_start = (b * nf + f) * out_cols
    noise_cols = lax.dynamic_slice_in_dim(noise[1], col_start, out_cols, 1).astype(jnp.float32)
    latent_cols = lax.dynamic_slice_in_dim(latents, col_start, out_cols, 1).astype(jnp.float32)
    return (done[0], done[1] - (noise_cols - latent_cols))


def attend_all(queries, key_rows, value_rows):
    passes, key_count = (key_rows.shape[0], key_rows.shape[1])
    local_heads = queries.shape[2]
    key_rows = key_rows.reshape(passes, key_count, local_heads, HD)
    value_rows = value_rows.reshape(passes, key_count, local_heads, HD)
    scores = jnp.einsum(
        "pqhd,prhd->pqhr", queries, key_rows, preferred_element_type=jnp.float32
    ) * HD ** (-0.5)
    softmax_w = jnp.exp(scores - jnp.max(scores, axis=-1, keepdims=True))
    mass = jnp.sum(softmax_w, axis=-1)
    mixed = jnp.einsum(
        "pqhr,prhd->pqhd",
        softmax_w.astype(jnp.bfloat16),
        value_rows,
        preferred_element_type=jnp.float32,
    )
    return (mixed / mass[..., None]).astype(jnp.bfloat16)


def normed(noisy_rows, gain_row, shift_row):
    mean_square = jnp.mean(noisy_rows * noisy_rows, axis=-1, keepdims=True)
    return (noisy_rows * lax.rsqrt(mean_square + EPSILON) * gain_row + shift_row).astype(
        jnp.bfloat16
    )


def gathered_body(latents, noise, time_index, cfg_pair, cond_table, gain, w_qkv, w_out):
    branch = lax.axis_index("branch")
    fsdp_count = lax.axis_size("fsdp")
    tok_rows = latents.shape[0]
    tokens = latents.astype(jnp.float32)
    noisy_main = noisy_mix(tokens, noise[0], time_index[0])
    own_noise = lax.dynamic_index_in_dim(noise, branch, 0, keepdims=False)
    own_index = lax.dynamic_index_in_dim(time_index, branch, 0, keepdims=False)
    noisy_own = noisy_mix(tokens, own_noise, own_index)
    cond_shift = table_row(cond_table, cfg_pair[0])
    second_row = lax.dynamic_index_in_dim(cfg_pair, 1 - branch, 0, keepdims=False)
    second_shift = table_row(cond_table, second_row)
    gain_row = gain[0]
    inputs = jnp.stack(
        [normed(noisy_main, gain_row, cond_shift), normed(noisy_own, gain_row, second_shift)]
    )
    weights = w_qkv[0]
    col_count = weights.shape[2]
    local_heads = col_count // HD
    projected = jnp.einsum(
        "ptd,jdc->pjtc",
        inputs,
        lax.all_gather(weights, "seq", axis=1, tiled=True),
        preferred_element_type=jnp.float32,
    ).astype(jnp.bfloat16)
    attn = attend_all(
        projected[:, 0].reshape(2, tok_rows, local_heads, HD),
        lax.all_gather(projected[:, 1], "seq", axis=1, tiled=True),
        lax.all_gather(projected[:, 2], "seq", axis=1, tiled=True),
    ).reshape(2, tok_rows, col_count)
    partial_value = jnp.einsum(
        "ptc,cd->ptd",
        attn,
        lax.all_gather(w_out[0], "seq", axis=1, tiled=True),
        preferred_element_type=jnp.float32,
    )
    width_all = partial_value.shape[2]
    half_width = width_all // (2 * fsdp_count)
    partial_value = (
        partial_value.reshape(2, tok_rows, 2, fsdp_count, half_width)
        .transpose(0, 1, 3, 2, 4)
        .reshape(2, tok_rows, width_all)
    )
    head_sums = lax.psum_scatter(
        partial_value.astype(jnp.bfloat16), "fsdp", scatter_dimension=2, tiled=True
    ).astype(jnp.float32)
    own_half = lax.dynamic_slice_in_dim(head_sums, branch * half_width, half_width, 2)
    give_half = lax.dynamic_slice_in_dim(head_sums, (1 - branch) * half_width, half_width, 2)
    partner_half = swap(give_half.astype(jnp.bfloat16), "branch").astype(jnp.float32)
    is_teacher = branch == 0
    teacher = jnp.where(is_teacher, own_half, partner_half)
    critic = jnp.where(is_teacher, partner_half, own_half)
    dmd_grad = critic[0] - (teacher[1] + GUIDANCE * (teacher[0] - teacher[1]))
    col_start = (branch * fsdp_count + lax.axis_index("fsdp")) * half_width
    noise_cols = lax.dynamic_slice_in_dim(noise[1], col_start, half_width, 1).astype(jnp.float32)
    latent_cols = lax.dynamic_slice_in_dim(latents, col_start, half_width, 1).astype(jnp.float32)
    return (dmd_grad, critic[1] - (noise_cols - latent_cols))


def solution(mesh):
    sizes = dict(mesh.shape)
    branches, seq, fsdp = sizes["branch"], sizes["seq"], sizes["fsdp"]

    def run(latents, noise, time_index, cfg_pair, cond_table, gain, w_qkv, w_out):
        local_heads = w_qkv.shape[3] // HD // fsdp
        outer = math.gcd(local_heads, seq)
        split = outer == branches * fsdp and seq == 2 * outer and branches == 2 and fsdp == 2
        if split:
            used = Mesh(
                mesh.devices.reshape(branches, outer, 2, fsdp),
                ("branch", "outer", "inner", "fsdp"),
            )
            body, along = split_body, ("outer", "inner")
        else:
            used, body, along = mesh, gathered_body, "seq"
        out = P(along, ("branch", "fsdp"))
        step = jax.shard_map(
            body,
            mesh=used,
            in_specs=(
                P(along, None),
                P(None, along, None),
                P(),
                P(),
                P(),
                P("branch", None),
                P("branch", None, along, "fsdp"),
                P("branch", "fsdp", along),
            ),
            out_specs=(out, out),
            check_vma=False,
        )
        return step(latents, noise, time_index, cfg_pair, cond_table, gain, w_qkv, w_out)

    return run
```

```python
import functools
import math

import jax
import jax.numpy as jnp
from jax import lax
from jax.experimental import pallas as pl
from jax.experimental.pallas import tpu as pltpu
from jax.sharding import Mesh
from jax.sharding import PartitionSpec as P


HD = 128
GUIDANCE = 3.5
EPSILON = 1e-06


def sigma_of(step_index):
    fraction = step_index.astype(jnp.float32) / 1000.0
    return 5.0 * fraction / (1.0 + 4.0 * fraction)


def noisy_mix(tokens, noise_rows, step_index):
    noise_level = sigma_of(step_index)
    return (1.0 - noise_level) * tokens + noise_level * noise_rows.astype(jnp.float32)


def table_row(cond_table, cond_row):
    one_hot = (jnp.arange(cond_table.shape[0], dtype=jnp.int32) == cond_row).astype(jnp.float32)
    return jnp.dot(one_hot, cond_table, precision=lax.Precision.HIGHEST)


def swap(x, axis):
    return lax.ppermute(x, axis, [(0, 1), (1, 0)])


def shift(x, axis, distance):
    size = lax.axis_size(axis)
    return lax.ppermute(x, axis, [(i, (i + distance) % size) for i in range(size)])


def prepare_kernel(b_ref, at_ref, time_ref, latents_ref, noise_ref, *refs):
    *out_refs, held_ref = refs
    _, width = latents_ref.shape
    blocks = at_ref.shape[0]
    step = jnp.full((1, HD), time_ref[b_ref[0]], jnp.int32)
    level = sigma_of(step)[:, :1]
    noisy = (1.0 - level) * latents_ref[...].astype(jnp.float32)
    noisy += level * noise_ref[0].astype(jnp.float32)
    mean_square = jnp.mean(noisy * noisy, axis=1, keepdims=True)
    held_ref[...] = noisy * lax.rsqrt(mean_square + EPSILON)
    size = width // blocks
    each = blocks // len(out_refs)
    for p in range(blocks):
        at = pl.multiple_of(at_ref[p] * size, HD)
        to = slice(p % each * size, (p % each + 1) * size)
        out_refs[p // each][:, to] = held_ref[:, pl.ds(at, size)].astype(jnp.bfloat16)


def prepare(b, order, time_index, latents, noise):
    tok, width = latents.shape
    tile = tok // 2 if tok % 32 == 0 else tok
    rows = pl.BlockSpec((tile, width), lambda t, *_: (t, 0))
    return pl.pallas_call(
        prepare_kernel,
        name="prepare",
        grid_spec=pltpu.PrefetchScalarGridSpec(
            num_scalar_prefetch=3,
            grid=(tok // tile,),
            in_specs=[rows, pl.BlockSpec((1, tile, width), lambda t, b, *_: (b[0], t, 0))],
            out_specs=[pl.BlockSpec((tile, width // 2), lambda t, *_: (t, 0))] * 2,
            scratch_shapes=[pltpu.VMEM((tile, width), jnp.float32)],
        ),
        out_shape=[jax.ShapeDtypeStruct((tok, width // 2), jnp.bfloat16)] * 2,
        cost_estimate=pl.CostEstimate(
            flops=6 * tok * width, transcendentals=tok, bytes_accessed=6 * tok * width
        ),
    )(b, order, time_index, latents, noise)


def gather_kernel(b_ref, at_ref, cfg_ref, z_ref, *refs):
    own_ref, *pieces, gain_ref, table_ref, x_ref, o_ref = refs
    tok = own_ref.shape[0]
    count = len(pieces) // 2 + 1
    z = z_ref[0]
    gain_row = gain_ref[...]
    shift_row = table_ref[pl.ds(cfg_ref[1 - b_ref[0]], 1), :]
    for k in range(count):
        if k == 0:
            rows = own_ref[...]
        else:
            rows = jnp.where(z + k < count, pieces[2 * k - 2][...], pieces[2 * k - 1][...])
        to = pl.ds(pl.multiple_of((z + k) % count * tok, tok), tok)
        x_ref[to, :] = rows
        o_ref[to, :] = (rows.astype(jnp.float32) * gain_row + shift_row).astype(jnp.bfloat16)


def affine_kernel(b_ref, at_ref, cfg_ref, own_ref, main_ref, gain_ref, table_ref, o_ref):
    main = jnp.where(b_ref[0] == 0, own_ref[...], main_ref[...]).astype(jnp.float32)
    cond = table_ref[pl.ds(cfg_ref[0], 1), :]
    o_ref[...] = (main * gain_ref[...] + cond).astype(jnp.bfloat16)


def columns(kernel, scalars, arrays, gain, table, rows, outputs):
    order = scalars[1]
    width = arrays[0].shape[1]
    size = width // order.shape[0]

    def block(height):
        return pl.BlockSpec((height, size), lambda p, *_: (0, p))

    def turned(height):
        return pl.BlockSpec((height, size), lambda p, b, at, *_: (0, at[p]))

    return pl.pallas_call(
        kernel,
        grid_spec=pltpu.PrefetchScalarGridSpec(
            num_scalar_prefetch=len(scalars),
            grid=(order.shape[0],),
            in_specs=[block(a.shape[0]) for a in arrays] + [turned(1), turned(table.shape[0])],
            out_specs=[block(rows)] * outputs,
        ),
        out_shape=[jax.ShapeDtypeStruct((rows, width), jnp.bfloat16)] * outputs,
        cost_estimate=pl.CostEstimate(
            flops=2 * rows * width, transcendentals=0, bytes_accessed=6 * rows * width
        ),
    )(*scalars, *arrays, gain, table)


def project_kernel(place_ref, *refs):
    inputs, blocks, (q_ref, kv_ref) = refs[:4], refs[4:-2], refs[-2:]
    totals = [None, None]
    for d in range(len(blocks) // 2):
        pair = blocks[2 * d : 2 * d + 2]
        weight = jnp.concatenate(
            [jnp.concatenate([w[j] for j in range(3)], axis=1) for w in pair], axis=0
        )
        depth = weight.shape[0]
        each = inputs[0].shape[1] // depth
        here = pl.ds(pl.multiple_of(place_ref[d] % each * depth, HD), depth)
        for p in range(2):
            mine, theirs = inputs[2 * p : 2 * p + 2]
            rows = jnp.where(place_ref[d] < each, mine[:, here], theirs[:, here])
            part = jnp.dot(rows, weight, preferred_element_type=jnp.float32)
            totals[p] = part if d == 0 else totals[p] + part
    for p in range(2):
        total = totals[p].astype(jnp.bfloat16)
        q_ref[p] = total[:, :HD]
        kv_ref[p] = total[:, HD:]


def project(inputs, places, weights, own_swapped, pieces, head):
    rows, half = inputs[0].shape
    width = 2 * half
    depth = weights.shape[1]
    tile = rows // 4 if rows % 64 == 0 else rows
    whole = pl.BlockSpec((3, depth, HD), lambda t, at: (0, 0, 0))
    return pl.pallas_call(
        project_kernel,
        name="project",
        grid_spec=pltpu.PrefetchScalarGridSpec(
            num_scalar_prefetch=1,
            grid=(rows // tile,),
            in_specs=[pl.BlockSpec((tile, half), lambda t, at: (t, 0))] * 4
            + [
                pl.BlockSpec((3, depth, HD), lambda t, at: (0, 0, at[at.shape[0] - 1] + head)),
                pl.BlockSpec((3, depth, HD), lambda t, at: (0, 0, head)),
            ]
            + [whole] * len(pieces),
            out_specs=[
                pl.BlockSpec((2, tile, HD), lambda t, at: (0, t, 0)),
                pl.BlockSpec((2, tile, 2 * HD), lambda t, at: (0, t, 0)),
            ],
        ),
        out_shape=[
            jax.ShapeDtypeStruct((2, rows, HD), jnp.bfloat16),
            jax.ShapeDtypeStruct((2, rows, 2 * HD), jnp.bfloat16),
        ],
        cost_estimate=pl.CostEstimate(
            flops=12 * rows * width * HD,
            transcendentals=0,
            bytes_accessed=2 * (2 * rows * (width + 3 * HD) + 3 * width * HD),
        ),
    )(places, *inputs, weights, own_swapped, *pieces)


def attend_kernel(b_ref, q_ref, own_ref, other_ref, o_ref, give_ref):
    dims = (((1,), (1,)), ((), ()))
    scale = HD ** (-0.5) * math.log2(math.e)
    tile = q_ref.shape[1]
    step, steps = pl.program_id(0), pl.num_programs(0)
    mixed = []
    for p in range(2):
        q, own, other = q_ref[p], own_ref[p], other_ref[p]
        s0 = lax.dot_general(q, own[:, :HD], dims, preferred_element_type=jnp.float32)
        s1 = lax.dot_general(q, other[:, :HD], dims, preferred_element_type=jnp.float32)
        peak = jnp.maximum(
            jnp.max(s0, axis=1, keepdims=True), jnp.max(s1, axis=1, keepdims=True)
        )
        p0 = jnp.exp2((s0 - peak) * scale)
        p1 = jnp.exp2((s1 - peak) * scale)
        mass = jnp.sum(p0, axis=1, keepdims=True) + jnp.sum(p1, axis=1, keepdims=True)
        total = jnp.dot(p0.astype(jnp.bfloat16), own[:, HD:], preferred_element_type=jnp.float32)
        total += jnp.dot(
            p1.astype(jnp.bfloat16), other[:, HD:], preferred_element_type=jnp.float32
        )
        mixed.append(total / mass)
    teacher = b_ref[0] == 0
    main = jnp.where(teacher, mixed[1] + GUIDANCE * (mixed[0] - mixed[1]), mixed[0])
    second = mixed[1].astype(jnp.bfloat16)
    o_ref[pl.ds(step * tile, tile), :] = main.astype(jnp.bfloat16)

    @pl.when(step < steps // 2)
    def _():
        give_ref[pl.ds(step * tile, tile), :] = second

    @pl.when(step >= steps // 2)
    def _():
        o_ref[pl.ds((step + steps // 2) * tile, tile), :] = second


def attend(b, q, own, other):
    passes, rows, _ = q.shape
    keys = own.shape[1] + other.shape[1]
    tile = rows // 4 if rows % 64 == 0 else rows // 2
    kv_spec = pl.BlockSpec((passes, own.shape[1], 2 * HD), lambda t, b: (0, 0, 0))
    return pl.pallas_call(
        attend_kernel,
        name="attend",
        grid_spec=pltpu.PrefetchScalarGridSpec(
            num_scalar_prefetch=1,
            grid=(rows // tile,),
            in_specs=[
                pl.BlockSpec((passes, tile, HD), lambda t, b: (0, t, 0)),
                kv_spec,
                kv_spec,
            ],
            out_specs=[
                pl.BlockSpec((rows * 3 // 2, HD), lambda t, b: (0, 0)),
                pl.BlockSpec((rows // 2, HD), lambda t, b: (0, 0)),
            ],
        ),
        out_shape=[
            jax.ShapeDtypeStruct((rows * 3 // 2, HD), jnp.bfloat16),
            jax.ShapeDtypeStruct((rows // 2, HD), jnp.bfloat16),
        ],
        cost_estimate=pl.CostEstimate(
            flops=4 * passes * rows * keys * HD,
            transcendentals=passes * rows * keys,
            bytes_accessed=2 * (2 * q.size + 2 * own.size),
        ),
    )(b, q, own, other)


def project_out_kernel(count, choices, first, at_ref, *refs):
    pieces, weights = refs[:count], refs[count : (1 + choices) * count]
    rows = jnp.concatenate([a[...] for a in pieces], axis=1)
    weight = jnp.concatenate([w[...] for w in weights[:count]], axis=0)
    if choices == 2:
        other = jnp.concatenate([w[...] for w in weights[count:]], axis=0)
        weight = jnp.where(at_ref[at_ref.shape[0] - 1] == 0, weight, other)
    total = jnp.dot(rows, weight, preferred_element_type=jnp.float32)
    refs[-1][...] = total if first else refs[-2][...] + total


def project_out(sets, tiles, places, choices, carry):
    tile = sets[0][1][0].shape[0] // 3
    each = len(sets[0][1]) // 2
    count = 2 * each * len(sets)
    width = choices[0][0].shape[1]
    lo, hi = tiles
    rows = (hi - lo) * tile
    first = carry is None

    def weight_spec(k, head):
        return pl.BlockSpec((HD, width), lambda t, at: (at[k] + head, 0))

    weight_specs = [weight_spec(k % each, head) for head, _ in sets for k in range(2 * each)]
    o_spec = pl.BlockSpec((tile, width), lambda t, at: (t, 0))
    return pl.pallas_call(
        functools.partial(project_out_kernel, count, len(choices), first),
        name="project_out",
        grid_spec=pltpu.PrefetchScalarGridSpec(
            num_scalar_prefetch=1,
            grid=(hi - lo,),
            in_specs=[pl.BlockSpec((tile, HD), lambda t, at: (t + lo, 0))] * count
            + weight_specs * len(choices)
            + ([] if first else [o_spec]),
            out_specs=o_spec,
        ),
        out_shape=jax.ShapeDtypeStruct((rows, width), jnp.float32),
        cost_estimate=pl.CostEstimate(
            flops=2 * rows * width * HD * count,
            transcendentals=0,
            bytes_accessed=2 * HD * count * (rows + width) + 8 * rows * width,
        ),
    )(
        places,
        *[piece for _, pieces in sets for piece in pieces],
        *[w for m, t in choices for w in ([m] * each + [t] * each) * len(sets)],
        *([] if first else [carry]),
    )


def split_body(*operands):
    return split_step(*operands)


def split_step(latents, noise, time_index, cfg_pair, cond_table, gain, w_qkv, w_out):
    b = lax.axis_index("branch")
    z = lax.axis_index("outer")
    y = lax.axis_index("inner")
    f = lax.axis_index("fsdp")
    nz = lax.axis_size("outer")
    nf = lax.axis_size("fsdp")
    tok, _ = latents.shape
    weights = w_qkv[0]
    _, cols = weights.shape[1:]
    head_count = cols // HD // nz

    span = head_count * HD
    own_swapped = swap(lax.dynamic_slice_in_dim(weights, z * span, span, 2), "inner")
    head_pieces = []
    for head in range(head_count):
        pieces = []
        for d in range(1, nz):
            start = (z + d) % nz * span + head * HD
            send = lax.dynamic_slice_in_dim(weights, start, HD, 2)
            received = shift(send, "outer", d)
            pieces += [received, swap(received, "inner")]
        head_pieces.append(pieces)
    from_z = jnp.stack([(z - d) % nz for d in range(nz)])
    places = jnp.concatenate([(from_z - 2 * f) % nz, (z * head_count)[None]]).astype(jnp.int32)

    which = b[None].astype(jnp.int32)
    order = jnp.stack(
        [(p // 2 + f * (nz // nf)) % nz * 2 + (y ^ (p % 2)) for p in range(2 * nz)]
    ).astype(jnp.int32)
    unit = prepare(which, order, time_index, latents, noise)
    ups = downs = [(unit[0], None)]
    for k in range(1, nz):
        up = lax.ppermute(ups[-1][0], "outer", [(i, i + 1) for i in range(k - 1, nz - 1)])
        down = lax.ppermute(downs[-1][0], "outer", [(i, i - 1) for i in range(1, nz - k + 1)])
        pairs = [(i * nf + j, i * nf + 1 - j) for i in range(nz) for j in range(nf)]
        ups = ups + [(up, lax.ppermute(up, ("outer", "fsdp"), pairs[k * nf :]))]
        downs = downs + [(down, lax.ppermute(down, ("outer", "fsdp"), pairs[: -k * nf]))]
    rows = nz * tok
    mains, seconds = [], []
    for side in range(2):
        part = order[side * nz : (side + 1) * nz]
        pieces = [unit[side]]
        for k in range(1, nz):
            pieces += [downs[k][side], ups[nz - k][side]]
        scalars = (which, part, cfg_pair)
        own_rows, second = columns(
            gather_kernel, (*scalars, z[None].astype(jnp.int32)), pieces, gain, cond_table, rows, 2
        )
        main_rows = lax.ppermute(own_rows, "branch", [(0, 1)])
        (main,) = columns(affine_kernel, scalars, [own_rows, main_rows], gain, cond_table, rows, 1)
        mains.append(main)
        seconds.append(second)
    inputs = (*mains, *seconds)

    out_here = w_out[0]
    out_width = out_here.shape[1]
    out_there = swap(out_here, "inner")
    out_mine = jnp.where(f == y, out_here, out_there)
    out_sent = jnp.where(f == y, out_there, out_here)
    out_theirs = swap(out_sent, "fsdp")
    out_own = (out_mine, out_theirs)
    out_critic = tuple(lax.ppermute(w, "branch", [(1, 0)]) for w in out_own)
    out_places = jnp.concatenate([from_z * head_count, b[None]]).astype(jnp.int32)

    sets = []
    for head in range(head_count):
        q, pair = project(inputs, places, weights, own_swapped, head_pieces[head], head)
        other = swap(pair, "inner")
        attn, give = attend(which, q, pair, other)
        taken = lax.ppermute(give, "branch", [(1, 0)])
        attn = lax.dynamic_update_slice(attn, jnp.where(b == 0, taken, attn[rows:]), (rows, 0))
        ours, across = [attn], [swap(attn, "fsdp")]
        for k in range(1, nz):
            ours.append(shift(attn, "outer", k))
            across.append(swap(ours[-1], "fsdp"))
        sets.append((head, ours + across))
    main_only, either = (out_own,), (out_critic, out_own)
    early = project_out(sets[:-1], (0, 2), out_places, main_only, None)
    early_own = project_out(sets[:-1], (2, 3), out_places, either, None)
    pred = project_out(sets[-1:], (0, 2), out_places, main_only, early)
    own_pred = project_out(sets[-1:], (2, 3), out_places, either, early_own)

    kept = lax.dynamic_slice_in_dim(pred, b * (rows // 2), rows // 2, 0)
    given = lax.dynamic_slice_in_dim(pred, (1 - b) * (rows // 2), rows // 2, 0)
    given = swap(given, "branch")
    dmd = jnp.where(b == 0, given - kept, kept - given)
    value = jnp.stack([dmd, own_pred]).astype(jnp.bfloat16)
    value = value.reshape(2, nz // 2, tok, out_width)
    received = []
    axes = ("branch", "outer", "fsdp")
    for k in range(nz // 2):
        pairs = []
        for bb in range(2):
            for zz in range(nz):
                for ff in range(nf):
                    to = bb * (nz // 2) + (ff + k) % (nz // 2)
                    source = (bb * nz + zz) * nf + ff
                    target = (zz // nf * nz + to) * nf + zz % nf
                    pairs.append((source, target))
        block = lax.dynamic_index_in_dim(value, (f + k) % (nz // 2), 1, keepdims=False)
        received.append(lax.ppermute(block, axes, pairs))
    swapped = z % (nz // 2) == 1
    first = jnp.where(swapped, received[1], received[0])
    second = jnp.where(swapped, received[0], received[1])
    done = jnp.concatenate([first, second], axis=2).astype(jnp.float32)
    out_cols = out_width * nf
    col_start = (b * nf + f) * out_cols
    noise_cols = lax.dynamic_slice_in_dim(noise[1], col_start, out_cols, 1).astype(jnp.float32)
    latent_cols = lax.dynamic_slice_in_dim(latents, col_start, out_cols, 1).astype(jnp.float32)
    return (done[0], done[1] - (noise_cols - latent_cols))


def attend_all(queries, key_rows, value_rows):
    passes, key_count = (key_rows.shape[0], key_rows.shape[1])
    local_heads = queries.shape[2]
    key_rows = key_rows.reshape(passes, key_count, local_heads, HD)
    value_rows = value_rows.reshape(passes, key_count, local_heads, HD)
    scores = jnp.einsum(
        "pqhd,prhd->pqhr", queries, key_rows, preferred_element_type=jnp.float32
    ) * HD ** (-0.5)
    softmax_w = jnp.exp(scores - jnp.max(scores, axis=-1, keepdims=True))
    mass = jnp.sum(softmax_w, axis=-1)
    mixed = jnp.einsum(
        "pqhr,prhd->pqhd",
        softmax_w.astype(jnp.bfloat16),
        value_rows,
        preferred_element_type=jnp.float32,
    )
    return (mixed / mass[..., None]).astype(jnp.bfloat16)


def normed(noisy_rows, gain_row, shift_row):
    mean_square = jnp.mean(noisy_rows * noisy_rows, axis=-1, keepdims=True)
    return (noisy_rows * lax.rsqrt(mean_square + EPSILON) * gain_row + shift_row).astype(
        jnp.bfloat16
    )


def gathered_body(latents, noise, time_index, cfg_pair, cond_table, gain, w_qkv, w_out):
    branch = lax.axis_index("branch")
    fsdp_count = lax.axis_size("fsdp")
    tok_rows = latents.shape[0]
    tokens = latents.astype(jnp.float32)
    noisy_main = noisy_mix(tokens, noise[0], time_index[0])
    own_noise = lax.dynamic_index_in_dim(noise, branch, 0, keepdims=False)
    own_index = lax.dynamic_index_in_dim(time_index, branch, 0, keepdims=False)
    noisy_own = noisy_mix(tokens, own_noise, own_index)
    cond_shift = table_row(cond_table, cfg_pair[0])
    second_row = lax.dynamic_index_in_dim(cfg_pair, 1 - branch, 0, keepdims=False)
    second_shift = table_row(cond_table, second_row)
    gain_row = gain[0]
    inputs = jnp.stack(
        [normed(noisy_main, gain_row, cond_shift), normed(noisy_own, gain_row, second_shift)]
    )
    weights = w_qkv[0]
    col_count = weights.shape[2]
    local_heads = col_count // HD
    projected = jnp.einsum(
        "ptd,jdc->pjtc",
        inputs,
        lax.all_gather(weights, "seq", axis=1, tiled=True),
        preferred_element_type=jnp.float32,
    ).astype(jnp.bfloat16)
    attn = attend_all(
        projected[:, 0].reshape(2, tok_rows, local_heads, HD),
        lax.all_gather(projected[:, 1], "seq", axis=1, tiled=True),
        lax.all_gather(projected[:, 2], "seq", axis=1, tiled=True),
    ).reshape(2, tok_rows, col_count)
    partial_value = jnp.einsum(
        "ptc,cd->ptd",
        attn,
        lax.all_gather(w_out[0], "seq", axis=1, tiled=True),
        preferred_element_type=jnp.float32,
    )
    width_all = partial_value.shape[2]
    half_width = width_all // (2 * fsdp_count)
    partial_value = (
        partial_value.reshape(2, tok_rows, 2, fsdp_count, half_width)
        .transpose(0, 1, 3, 2, 4)
        .reshape(2, tok_rows, width_all)
    )
    head_sums = lax.psum_scatter(
        partial_value.astype(jnp.bfloat16), "fsdp", scatter_dimension=2, tiled=True
    ).astype(jnp.float32)
    own_half = lax.dynamic_slice_in_dim(head_sums, branch * half_width, half_width, 2)
    give_half = lax.dynamic_slice_in_dim(head_sums, (1 - branch) * half_width, half_width, 2)
    partner_half = swap(give_half.astype(jnp.bfloat16), "branch").astype(jnp.float32)
    is_teacher = branch == 0
    teacher = jnp.where(is_teacher, own_half, partner_half)
    critic = jnp.where(is_teacher, partner_half, own_half)
    dmd_grad = critic[0] - (teacher[1] + GUIDANCE * (teacher[0] - teacher[1]))
    col_start = (branch * fsdp_count + lax.axis_index("fsdp")) * half_width
    noise_cols = lax.dynamic_slice_in_dim(noise[1], col_start, half_width, 1).astype(jnp.float32)
    latent_cols = lax.dynamic_slice_in_dim(latents, col_start, half_width, 1).astype(jnp.float32)
    return (dmd_grad, critic[1] - (noise_cols - latent_cols))


def solution(mesh):
    sizes = dict(mesh.shape)
    branches, seq, fsdp = sizes["branch"], sizes["seq"], sizes["fsdp"]

    def run(latents, noise, time_index, cfg_pair, cond_table, gain, w_qkv, w_out):
        local_heads = w_qkv.shape[3] // HD // fsdp
        outer = math.gcd(local_heads, seq)
        split = outer == branches * fsdp and seq == 2 * outer and branches == 2 and fsdp == 2
        if split:
            used = Mesh(
                mesh.devices.reshape(branches, outer, 2, fsdp),
                ("branch", "outer", "inner", "fsdp"),
            )
            body, along = split_body, ("outer", "inner")
        else:
            used, body, along = mesh, gathered_body, "seq"
        out = P(along, ("branch", "fsdp"))
        step = jax.shard_map(
            body,
            mesh=used,
            in_specs=(
                P(along, None),
                P(None, along, None),
                P(),
                P(),
                P(),
                P("branch", None),
                P("branch", None, along, "fsdp"),
                P("branch", "fsdp", along),
            ),
            out_specs=(out, out),
            check_vma=False,
        )
        return step(latents, noise, time_index, cfg_pair, cond_table, gain, w_qkv, w_out)

    return run
```

```python
import functools
import math

import jax
import jax.numpy as jnp
from jax import lax
from jax.experimental import pallas as pl
from jax.experimental.pallas import tpu as pltpu
from jax.sharding import Mesh
from jax.sharding import PartitionSpec as P


HD = 128
GUIDANCE = 3.5
EPSILON = 1e-06


def sigma_of(step_index):
    fraction = step_index.astype(jnp.float32) / 1000.0
    return 5.0 * fraction / (1.0 + 4.0 * fraction)


def noisy_mix(tokens, noise_rows, step_index):
    noise_level = sigma_of(step_index)
    return (1.0 - noise_level) * tokens + noise_level * noise_rows.astype(jnp.float32)


def table_row(cond_table, cond_row):
    one_hot = (jnp.arange(cond_table.shape[0], dtype=jnp.int32) == cond_row).astype(jnp.float32)
    return jnp.dot(one_hot, cond_table, precision=lax.Precision.HIGHEST)


def swap(x, axis):
    return lax.ppermute(x, axis, [(0, 1), (1, 0)])


def shift(x, axis, distance):
    size = lax.axis_size(axis)
    return lax.ppermute(x, axis, [(i, (i + distance) % size) for i in range(size)])


def prepare_kernel(b_ref, at_ref, time_ref, latents_ref, noise_ref, *refs):
    *out_refs, held_ref = refs
    _, width = latents_ref.shape
    blocks = at_ref.shape[0]
    step = jnp.full((1, HD), time_ref[b_ref[0]], jnp.int32)
    level = sigma_of(step)[:, :1]
    noisy = (1.0 - level) * latents_ref[...].astype(jnp.float32)
    noisy += level * noise_ref[0].astype(jnp.float32)
    mean_square = jnp.mean(noisy * noisy, axis=1, keepdims=True)
    held_ref[...] = noisy * lax.rsqrt(mean_square + EPSILON)
    size = width // blocks
    each = blocks // len(out_refs)
    for p in range(blocks):
        at = pl.multiple_of(at_ref[p] * size, HD)
        to = slice(p % each * size, (p % each + 1) * size)
        out_refs[p // each][:, to] = held_ref[:, pl.ds(at, size)].astype(jnp.bfloat16)


def prepare(b, order, time_index, latents, noise):
    tok, width = latents.shape
    tile = tok // 2 if tok % 32 == 0 else tok
    rows = pl.BlockSpec((tile, width), lambda t, *_: (t, 0))
    return pl.pallas_call(
        prepare_kernel,
        name="prepare",
        grid_spec=pltpu.PrefetchScalarGridSpec(
            num_scalar_prefetch=3,
            grid=(tok // tile,),
            in_specs=[rows, pl.BlockSpec((1, tile, width), lambda t, b, *_: (b[0], t, 0))],
            out_specs=[pl.BlockSpec((tile, width // 2), lambda t, *_: (t, 0))] * 2,
            scratch_shapes=[pltpu.VMEM((tile, width), jnp.float32)],
        ),
        out_shape=[jax.ShapeDtypeStruct((tok, width // 2), jnp.bfloat16)] * 2,
        cost_estimate=pl.CostEstimate(
            flops=6 * tok * width, transcendentals=tok, bytes_accessed=6 * tok * width
        ),
    )(b, order, time_index, latents, noise)


def gather_kernel(b_ref, at_ref, cfg_ref, z_ref, *refs):
    own_ref, *pieces, gain_ref, table_ref, x_ref, o_ref = refs
    tok = own_ref.shape[0]
    count = len(pieces) // 2 + 1
    z = z_ref[0]
    gain_row = gain_ref[...]
    shift_row = table_ref[pl.ds(cfg_ref[1 - b_ref[0]], 1), :]
    for k in range(count):
        if k == 0:
            rows = own_ref[...]
        else:
            rows = jnp.where(z + k < count, pieces[2 * k - 2][...], pieces[2 * k - 1][...])
        to = pl.ds(pl.multiple_of((z + k) % count * tok, tok), tok)
        x_ref[to, :] = rows
        o_ref[to, :] = (rows.astype(jnp.float32) * gain_row + shift_row).astype(jnp.bfloat16)


def affine_kernel(b_ref, at_ref, cfg_ref, own_ref, main_ref, gain_ref, table_ref, o_ref):
    main = jnp.where(b_ref[0] == 0, own_ref[...], main_ref[...]).astype(jnp.float32)
    cond = table_ref[pl.ds(cfg_ref[0], 1), :]
    o_ref[...] = (main * gain_ref[...] + cond).astype(jnp.bfloat16)


def columns(kernel, scalars, arrays, gain, table, rows, outputs):
    order = scalars[1]
    width = arrays[0].shape[1]
    size = width // order.shape[0]

    def block(height):
        return pl.BlockSpec((height, size), lambda p, *_: (0, p))

    def turned(height):
        return pl.BlockSpec((height, size), lambda p, b, at, *_: (0, at[p]))

    return pl.pallas_call(
        kernel,
        grid_spec=pltpu.PrefetchScalarGridSpec(
            num_scalar_prefetch=len(scalars),
            grid=(order.shape[0],),
            in_specs=[block(a.shape[0]) for a in arrays] + [turned(1), turned(table.shape[0])],
            out_specs=[block(rows)] * outputs,
        ),
        out_shape=[jax.ShapeDtypeStruct((rows, width), jnp.bfloat16)] * outputs,
        cost_estimate=pl.CostEstimate(
            flops=2 * rows * width, transcendentals=0, bytes_accessed=6 * rows * width
        ),
    )(*scalars, *arrays, gain, table)


def project_kernel(place_ref, *refs):
    inputs, blocks, (q_ref, kv_ref) = refs[:4], refs[4:-2], refs[-2:]
    totals = [None, None]
    for d in range(len(blocks) // 2):
        pair = blocks[2 * d : 2 * d + 2]
        weight = jnp.concatenate(
            [jnp.concatenate([w[j] for j in range(3)], axis=1) for w in pair], axis=0
        )
        depth = weight.shape[0]
        each = inputs[0].shape[1] // depth
        here = pl.ds(pl.multiple_of(place_ref[d] % each * depth, HD), depth)
        for p in range(2):
            mine, theirs = inputs[2 * p : 2 * p + 2]
            rows = jnp.where(place_ref[d] < each, mine[:, here], theirs[:, here])
            part = jnp.dot(rows, weight, preferred_element_type=jnp.float32)
            totals[p] = part if d == 0 else totals[p] + part
    for p in range(2):
        total = totals[p].astype(jnp.bfloat16)
        q_ref[p] = total[:, :HD]
        kv_ref[p] = total[:, HD:]


def project(inputs, places, weights, own_swapped, pieces, head):
    rows, half = inputs[0].shape
    width = 2 * half
    depth = weights.shape[1]
    tile = rows // 4 if rows % 64 == 0 else rows
    whole = pl.BlockSpec((3, depth, HD), lambda t, at: (0, 0, 0))
    return pl.pallas_call(
        project_kernel,
        name="project",
        grid_spec=pltpu.PrefetchScalarGridSpec(
            num_scalar_prefetch=1,
            grid=(rows // tile,),
            in_specs=[pl.BlockSpec((tile, half), lambda t, at: (t, 0))] * 4
            + [
                pl.BlockSpec((3, depth, HD), lambda t, at: (0, 0, at[at.shape[0] - 1] + head)),
                pl.BlockSpec((3, depth, HD), lambda t, at: (0, 0, head)),
            ]
            + [whole] * len(pieces),
            out_specs=[
                pl.BlockSpec((2, tile, HD), lambda t, at: (0, t, 0)),
                pl.BlockSpec((2, tile, 2 * HD), lambda t, at: (0, t, 0)),
            ],
        ),
        out_shape=[
            jax.ShapeDtypeStruct((2, rows, HD), jnp.bfloat16),
            jax.ShapeDtypeStruct((2, rows, 2 * HD), jnp.bfloat16),
        ],
        cost_estimate=pl.CostEstimate(
            flops=12 * rows * width * HD,
            transcendentals=0,
            bytes_accessed=2 * (2 * rows * (width + 3 * HD) + 3 * width * HD),
        ),
    )(places, *inputs, weights, own_swapped, *pieces)


def attend_kernel(b_ref, q_ref, own_ref, other_ref, o_ref, give_ref):
    dims = (((1,), (1,)), ((), ()))
    scale = HD ** (-0.5) * math.log2(math.e)
    tile = q_ref.shape[1]
    step, steps = pl.program_id(0), pl.num_programs(0)
    mixed = []
    for p in range(2):
        q, own, other = q_ref[p], own_ref[p], other_ref[p]
        s0 = lax.dot_general(q, own[:, :HD], dims, preferred_element_type=jnp.float32)
        s1 = lax.dot_general(q, other[:, :HD], dims, preferred_element_type=jnp.float32)
        peak = jnp.maximum(
            jnp.max(s0, axis=1, keepdims=True), jnp.max(s1, axis=1, keepdims=True)
        )
        p0 = jnp.exp2((s0 - peak) * scale)
        p1 = jnp.exp2((s1 - peak) * scale)
        mass = jnp.sum(p0, axis=1, keepdims=True) + jnp.sum(p1, axis=1, keepdims=True)
        total = jnp.dot(p0.astype(jnp.bfloat16), own[:, HD:], preferred_element_type=jnp.float32)
        total += jnp.dot(
            p1.astype(jnp.bfloat16), other[:, HD:], preferred_element_type=jnp.float32
        )
        mixed.append(total / mass)
    teacher = b_ref[0] == 0
    main = jnp.where(teacher, mixed[1] + GUIDANCE * (mixed[0] - mixed[1]), mixed[0])
    second = mixed[1].astype(jnp.bfloat16)
    o_ref[pl.ds(step * tile, tile), :] = main.astype(jnp.bfloat16)

    @pl.when(step < steps // 2)
    def _():
        give_ref[pl.ds(step * tile, tile), :] = second

    @pl.when(step >= steps // 2)
    def _():
        o_ref[pl.ds((step + steps // 2) * tile, tile), :] = second


def attend(b, q, own, other):
    passes, rows, _ = q.shape
    keys = own.shape[1] + other.shape[1]
    tile = rows // 4 if rows % 64 == 0 else rows // 2
    kv_spec = pl.BlockSpec((passes, own.shape[1], 2 * HD), lambda t, b: (0, 0, 0))
    return pl.pallas_call(
        attend_kernel,
        name="attend",
        grid_spec=pltpu.PrefetchScalarGridSpec(
            num_scalar_prefetch=1,
            grid=(rows // tile,),
            in_specs=[
                pl.BlockSpec((passes, tile, HD), lambda t, b: (0, t, 0)),
                kv_spec,
                kv_spec,
            ],
            out_specs=[
                pl.BlockSpec((rows * 3 // 2, HD), lambda t, b: (0, 0)),
                pl.BlockSpec((rows // 2, HD), lambda t, b: (0, 0)),
            ],
        ),
        out_shape=[
            jax.ShapeDtypeStruct((rows * 3 // 2, HD), jnp.bfloat16),
            jax.ShapeDtypeStruct((rows // 2, HD), jnp.bfloat16),
        ],
        cost_estimate=pl.CostEstimate(
            flops=4 * passes * rows * keys * HD,
            transcendentals=passes * rows * keys,
            bytes_accessed=2 * (2 * q.size + 2 * own.size),
        ),
    )(b, q, own, other)


def project_out_kernel(count, choices, first, split, at_ref, *refs):
    pieces, weights = refs[:count], refs[count : (1 + choices) * count]
    rows = jnp.concatenate([a[...] for a in pieces], axis=1)
    weight = jnp.concatenate([w[...] for w in weights[:count]], axis=0)
    if choices == 2:
        other = jnp.concatenate([w[...] for w in weights[count:]], axis=0)
        weight = jnp.where(at_ref[at_ref.shape[0] - 1] == 0, weight, other)
    total = jnp.dot(rows, weight, preferred_element_type=jnp.float32)
    if not first:
        total = refs[-3 if split else -2][...] + total
    if not split:
        refs[-1][...] = total
        return
    kept = pl.program_id(0) == at_ref[at_ref.shape[0] - 1]

    @pl.when(kept)
    def _():
        refs[-2][...] = total

    @pl.when(jnp.logical_not(kept))
    def _():
        refs[-1][...] = total


def project_out(sets, tiles, places, choices, carry, split=False):
    tile = sets[0][1][0].shape[0] // 3
    each = len(sets[0][1]) // 2
    count = 2 * each * len(sets)
    width = choices[0][0].shape[1]
    lo, hi = tiles
    rows = (hi - lo) * tile
    first = carry is None

    def weight_spec(k, head):
        return pl.BlockSpec((HD, width), lambda t, at: (at[k] + head, 0))

    weight_specs = [weight_spec(k % each, head) for head, _ in sets for k in range(2 * each)]
    o_spec = pl.BlockSpec((tile, width), lambda t, at: (t, 0))
    return pl.pallas_call(
        functools.partial(project_out_kernel, count, len(choices), first, split),
        name="project_out",
        grid_spec=pltpu.PrefetchScalarGridSpec(
            num_scalar_prefetch=1,
            grid=(hi - lo,),
            in_specs=[pl.BlockSpec((tile, HD), lambda t, at: (t + lo, 0))] * count
            + weight_specs * len(choices)
            + ([] if first else [o_spec]),
            out_specs=[pl.BlockSpec((tile, width), lambda t, at: (0, 0))] * 2
            if split
            else o_spec,
        ),
        out_shape=[jax.ShapeDtypeStruct((tile, width), jnp.float32)] * 2
        if split
        else jax.ShapeDtypeStruct((rows, width), jnp.float32),
        cost_estimate=pl.CostEstimate(
            flops=2 * rows * width * HD * count,
            transcendentals=0,
            bytes_accessed=2 * HD * count * (rows + width) + 8 * rows * width,
        ),
    )(
        places,
        *[piece for _, pieces in sets for piece in pieces],
        *[w for m, t in choices for w in ([m] * each + [t] * each) * len(sets)],
        *([] if first else [carry]),
    )


def split_body(*operands):
    return split_step(*operands)


def split_step(latents, noise, time_index, cfg_pair, cond_table, gain, w_qkv, w_out):
    b = lax.axis_index("branch")
    z = lax.axis_index("outer")
    y = lax.axis_index("inner")
    f = lax.axis_index("fsdp")
    nz = lax.axis_size("outer")
    nf = lax.axis_size("fsdp")
    tok, _ = latents.shape
    weights = w_qkv[0]
    _, cols = weights.shape[1:]
    head_count = cols // HD // nz

    span = head_count * HD
    own_swapped = swap(lax.dynamic_slice_in_dim(weights, z * span, span, 2), "inner")
    head_pieces = []
    for head in range(head_count):
        pieces = []
        for d in range(1, nz):
            start = (z + d) % nz * span + head * HD
            send = lax.dynamic_slice_in_dim(weights, start, HD, 2)
            received = shift(send, "outer", d)
            pieces += [received, swap(received, "inner")]
        head_pieces.append(pieces)
    from_z = jnp.stack([(z - d) % nz for d in range(nz)])
    places = jnp.concatenate([(from_z - 2 * f) % nz, (z * head_count)[None]]).astype(jnp.int32)

    which = b[None].astype(jnp.int32)
    order = jnp.stack(
        [(p // 2 + f * (nz // nf)) % nz * 2 + (y ^ (p % 2)) for p in range(2 * nz)]
    ).astype(jnp.int32)
    unit = prepare(which, order, time_index, latents, noise)
    ups = downs = [(unit[0], None)]
    for k in range(1, nz):
        up = lax.ppermute(ups[-1][0], "outer", [(i, i + 1) for i in range(k - 1, nz - 1)])
        down = lax.ppermute(downs[-1][0], "outer", [(i, i - 1) for i in range(1, nz - k + 1)])
        pairs = [(i * nf + j, i * nf + 1 - j) for i in range(nz) for j in range(nf)]
        ups = ups + [(up, lax.ppermute(up, ("outer", "fsdp"), pairs[k * nf :]))]
        downs = downs + [(down, lax.ppermute(down, ("outer", "fsdp"), pairs[: -k * nf]))]
    rows = nz * tok
    mains, seconds = [], []
    for side in range(2):
        part = order[side * nz : (side + 1) * nz]
        pieces = [unit[side]]
        for k in range(1, nz):
            pieces += [downs[k][side], ups[nz - k][side]]
        scalars = (which, part, cfg_pair)
        own_rows, second = columns(
            gather_kernel, (*scalars, z[None].astype(jnp.int32)), pieces, gain, cond_table, rows, 2
        )
        main_rows = lax.ppermute(own_rows, "branch", [(0, 1)])
        (main,) = columns(affine_kernel, scalars, [own_rows, main_rows], gain, cond_table, rows, 1)
        mains.append(main)
        seconds.append(second)
    inputs = (*mains, *seconds)

    out_here = w_out[0]
    out_width = out_here.shape[1]
    out_there = swap(out_here, "inner")
    out_mine = jnp.where(f == y, out_here, out_there)
    out_sent = jnp.where(f == y, out_there, out_here)
    out_theirs = swap(out_sent, "fsdp")
    out_own = (out_mine, out_theirs)
    out_critic = tuple(lax.ppermute(w, "branch", [(1, 0)]) for w in out_own)
    out_places = jnp.concatenate([from_z * head_count, b[None]]).astype(jnp.int32)

    sets = []
    for head in range(head_count):
        q, pair = project(inputs, places, weights, own_swapped, head_pieces[head], head)
        other = swap(pair, "inner")
        attn, give = attend(which, q, pair, other)
        taken = lax.ppermute(give, "branch", [(1, 0)])
        attn = lax.dynamic_update_slice(attn, jnp.where(b == 0, taken, attn[rows:]), (rows, 0))
        ours, across = [attn], [swap(attn, "fsdp")]
        for k in range(1, nz):
            ours.append(shift(attn, "outer", k))
            across.append(swap(ours[-1], "fsdp"))
        sets.append((head, ours + across))
    main_only, either = (out_own,), (out_critic, out_own)
    early = project_out(sets[:-1], (0, 2), out_places, main_only, None)
    early_own = project_out(sets[:-1], (2, 3), out_places, either, None)
    kept, given = project_out(sets[-1:], (0, 2), out_places, main_only, early, split=True)
    own_pred = project_out(sets[-1:], (2, 3), out_places, either, early_own)

    given = swap(given, "branch")
    dmd = jnp.where(b == 0, given - kept, kept - given)
    value = jnp.stack([dmd, own_pred]).astype(jnp.bfloat16)
    value = value.reshape(2, nz // 2, tok, out_width)
    received = []
    axes = ("branch", "outer", "fsdp")
    for k in range(nz // 2):
        pairs = []
        for bb in range(2):
            for zz in range(nz):
                for ff in range(nf):
                    to = bb * (nz // 2) + (ff + k) % (nz // 2)
                    source = (bb * nz + zz) * nf + ff
                    target = (zz // nf * nz + to) * nf + zz % nf
                    pairs.append((source, target))
        block = lax.dynamic_index_in_dim(value, (f + k) % (nz // 2), 1, keepdims=False)
        received.append(lax.ppermute(block, axes, pairs))
    swapped = z % (nz // 2) == 1
    first = jnp.where(swapped, received[1], received[0])
    second = jnp.where(swapped, received[0], received[1])
    done = jnp.concatenate([first, second], axis=2).astype(jnp.float32)
    out_cols = out_width * nf
    col_start = (b * nf + f) * out_cols
    noise_cols = lax.dynamic_slice_in_dim(noise[1], col_start, out_cols, 1).astype(jnp.float32)
    latent_cols = lax.dynamic_slice_in_dim(latents, col_start, out_cols, 1).astype(jnp.float32)
    return (done[0], done[1] - (noise_cols - latent_cols))


def attend_all(queries, key_rows, value_rows):
    passes, key_count = (key_rows.shape[0], key_rows.shape[1])
    local_heads = queries.shape[2]
    key_rows = key_rows.reshape(passes, key_count, local_heads, HD)
    value_rows = value_rows.reshape(passes, key_count, local_heads, HD)
    scores = jnp.einsum(
        "pqhd,prhd->pqhr", queries, key_rows, preferred_element_type=jnp.float32
    ) * HD ** (-0.5)
    softmax_w = jnp.exp(scores - jnp.max(scores, axis=-1, keepdims=True))
    mass = jnp.sum(softmax_w, axis=-1)
    mixed = jnp.einsum(
        "pqhr,prhd->pqhd",
        softmax_w.astype(jnp.bfloat16),
        value_rows,
        preferred_element_type=jnp.float32,
    )
    return (mixed / mass[..., None]).astype(jnp.bfloat16)


def normed(noisy_rows, gain_row, shift_row):
    mean_square = jnp.mean(noisy_rows * noisy_rows, axis=-1, keepdims=True)
    return (noisy_rows * lax.rsqrt(mean_square + EPSILON) * gain_row + shift_row).astype(
        jnp.bfloat16
    )


def gathered_body(latents, noise, time_index, cfg_pair, cond_table, gain, w_qkv, w_out):
    branch = lax.axis_index("branch")
    fsdp_count = lax.axis_size("fsdp")
    tok_rows = latents.shape[0]
    tokens = latents.astype(jnp.float32)
    noisy_main = noisy_mix(tokens, noise[0], time_index[0])
    own_noise = lax.dynamic_index_in_dim(noise, branch, 0, keepdims=False)
    own_index = lax.dynamic_index_in_dim(time_index, branch, 0, keepdims=False)
    noisy_own = noisy_mix(tokens, own_noise, own_index)
    cond_shift = table_row(cond_table, cfg_pair[0])
    second_row = lax.dynamic_index_in_dim(cfg_pair, 1 - branch, 0, keepdims=False)
    second_shift = table_row(cond_table, second_row)
    gain_row = gain[0]
    inputs = jnp.stack(
        [normed(noisy_main, gain_row, cond_shift), normed(noisy_own, gain_row, second_shift)]
    )
    weights = w_qkv[0]
    col_count = weights.shape[2]
    local_heads = col_count // HD
    projected = jnp.einsum(
        "ptd,jdc->pjtc",
        inputs,
        lax.all_gather(weights, "seq", axis=1, tiled=True),
        preferred_element_type=jnp.float32,
    ).astype(jnp.bfloat16)
    attn = attend_all(
        projected[:, 0].reshape(2, tok_rows, local_heads, HD),
        lax.all_gather(projected[:, 1], "seq", axis=1, tiled=True),
        lax.all_gather(projected[:, 2], "seq", axis=1, tiled=True),
    ).reshape(2, tok_rows, col_count)
    partial_value = jnp.einsum(
        "ptc,cd->ptd",
        attn,
        lax.all_gather(w_out[0], "seq", axis=1, tiled=True),
        preferred_element_type=jnp.float32,
    )
    width_all = partial_value.shape[2]
    half_width = width_all // (2 * fsdp_count)
    partial_value = (
        partial_value.reshape(2, tok_rows, 2, fsdp_count, half_width)
        .transpose(0, 1, 3, 2, 4)
        .reshape(2, tok_rows, width_all)
    )
    head_sums = lax.psum_scatter(
        partial_value.astype(jnp.bfloat16), "fsdp", scatter_dimension=2, tiled=True
    ).astype(jnp.float32)
    own_half = lax.dynamic_slice_in_dim(head_sums, branch * half_width, half_width, 2)
    give_half = lax.dynamic_slice_in_dim(head_sums, (1 - branch) * half_width, half_width, 2)
    partner_half = swap(give_half.astype(jnp.bfloat16), "branch").astype(jnp.float32)
    is_teacher = branch == 0
    teacher = jnp.where(is_teacher, own_half, partner_half)
    critic = jnp.where(is_teacher, partner_half, own_half)
    dmd_grad = critic[0] - (teacher[1] + GUIDANCE * (teacher[0] - teacher[1]))
    col_start = (branch * fsdp_count + lax.axis_index("fsdp")) * half_width
    noise_cols = lax.dynamic_slice_in_dim(noise[1], col_start, half_width, 1).astype(jnp.float32)
    latent_cols = lax.dynamic_slice_in_dim(latents, col_start, half_width, 1).astype(jnp.float32)
    return (dmd_grad, critic[1] - (noise_cols - latent_cols))


def solution(mesh):
    sizes = dict(mesh.shape)
    branches, seq, fsdp = sizes["branch"], sizes["seq"], sizes["fsdp"]

    def run(latents, noise, time_index, cfg_pair, cond_table, gain, w_qkv, w_out):
        local_heads = w_qkv.shape[3] // HD // fsdp
        outer = math.gcd(local_heads, seq)
        split = outer == branches * fsdp and seq == 2 * outer and branches == 2 and fsdp == 2
        if split:
            used = Mesh(
                mesh.devices.reshape(branches, outer, 2, fsdp),
                ("branch", "outer", "inner", "fsdp"),
            )
            body, along = split_body, ("outer", "inner")
        else:
            used, body, along = mesh, gathered_body, "seq"
        out = P(along, ("branch", "fsdp"))
        step = jax.shard_map(
            body,
            mesh=used,
            in_specs=(
                P(along, None),
                P(None, along, None),
                P(),
                P(),
                P(),
                P("branch", None),
                P("branch", None, along, "fsdp"),
                P("branch", "fsdp", along),
            ),
            out_specs=(out, out),
            check_vma=False,
        )
        return step(latents, noise, time_index, cfg_pair, cond_table, gain, w_qkv, w_out)

    return run
```
